256 devices in a mesh: head: 4 (over x), seq: 64 (over z, y, core).
Axes of the slice: x: 4, y: 4, z: 8, core: 2. Of those that a mesh axis runs over, the one named last changes fastest.
Arguments:
- queries: bfloat16 [16384, 3072], P(('head', 'seq')), may hold values from -6 to 6
- key_rows: bfloat16 [49152, 3072], P('seq', 'head'), may hold values from -6 to 6
- values: bfloat16 [49152, 3072], P('seq', 'head'), may hold values from -6 to 6
- w_out: bfloat16 [3072, 6144], P('head'), may hold values from -1.1953125 to 1.1953125
- picked: int32 [256, 24], replicated, may hold values from 0 to 767, as said below
- counts: int32 [256], replicated, may hold values from 8 to 24
- tile_home: int32 [768], replicated, may hold values from 0 to 767, as said below
Outputs:
- layer_out: bfloat16 [16384, 6144], P(('head', 'seq'))
The draws below stay inside these ranges and needn't reach their ends.
Inputs may be any that keep to these rules, and one draw needn't show every extreme that they name: `picked`: query tiles j with the same j modulo the number of devices along seq form a group. The used entries of one group are distinct key tiles; key tile t is stored on owner tile_home[t] // 12, and at most 2 used entries of one group are stored on one owner, exactly 2 for some owner in every group. `tile_home`: A permutation of the key tiles.
All inputs are finite; a program needn't handle non-finite values.
Results may differ from the reference program's by a relative error of at most 0.009.
Values may be sent and summed in bfloat16 or wider, within the bound.
No kernel may reach another device: no remote copies, remote signals or barrier semaphores. Data moves between devices by JAX's collectives and lax.ppermute only.
A program may use at most 128 MiB of HBM per device.

```python
import jax
import jax.numpy as jnp
from jax import lax

D = 6144
HD = 128
TILE_TOKENS = 64
KT_DEV = 12
MAXSEL = 24
MINSEL = 8
QUERY_FEATURES = 3072
NQT = 256
NQ = 16384
NKT = 768
KEY_TOKENS = 49152
CAP = 2
N_HEAD = 4


def shared_home(key):
    return jax.random.permutation(jax.random.fold_in(key, 11), NKT).astype(jnp.int32)


def draw_tile_home(key, part):
    return shared_home(key)


def draw_picked(key, part):
    home_map = shared_home(key)
    inverse = jnp.zeros((NKT,), jnp.int32).at[home_map].set(jnp.arange(NKT, dtype=jnp.int32))
    seq_count = NKT // KT_DEV
    group_tiles = NQT // seq_count
    slot_count = seq_count * CAP
    base_key = jax.random.fold_in(key, 23)
    hot_owner = jax.random.randint(jax.random.fold_in(base_key, 1), (seq_count,), 0, seq_count).astype(jnp.int32)
    random_part = jax.random.randint(jax.random.fold_in(base_key, 2), (seq_count, slot_count), 0, 1 << 20).astype(jnp.int32)
    slot_ids = jnp.arange(slot_count, dtype=jnp.int32)
    ranking = random_part * slot_count + slot_ids[None, :]
    ranking = ranking + jnp.where(slot_ids[None, :] // CAP == hot_owner[:, None], 1 << 29, 0).astype(jnp.int32)
    slot_order = jnp.argsort(-ranking, axis=1).astype(jnp.int32)[:, :group_tiles * MAXSEL]
    owner_of = slot_order // CAP
    slot_within = slot_order % CAP
    offset = jax.random.randint(jax.random.fold_in(base_key, 3), (seq_count, seq_count), 0, KT_DEV).astype(jnp.int32)
    start_at = jnp.take_along_axis(offset, owner_of, axis=1)
    stored = owner_of * KT_DEV + (start_at + slot_within) % KT_DEV
    chosen = inverse[stored]
    chosen = chosen.reshape(seq_count, MAXSEL, group_tiles).transpose(2, 0, 1).reshape(NQT, MAXSEL)
    return chosen.astype(jnp.int32)


def draw_counts(key, part):
    sampled_tiles = jax.random.randint(jax.random.fold_in(key, 31), (NQT,), MINSEL, MAXSEL + 1).astype(jnp.int32)
    return sampled_tiles.at[0].set(MAXSEL).at[1].set(MINSEL)


def draw_queries(key, part):
    sampled_tiles = jnp.clip(1.5 * jax.random.normal(jax.random.fold_in(key, 5), (NQ, QUERY_FEATURES), jnp.float32), -6.0, 6.0)
    return sampled_tiles.astype(jnp.bfloat16)


def draw_key_rows(key, part):
    sampled_tiles = jnp.clip(jax.random.normal(jax.random.fold_in(key, 7), (KEY_TOKENS, QUERY_FEATURES), jnp.float32), -6.0, 6.0)
    return sampled_tiles.astype(jnp.bfloat16)


def block_scale(rng, extent, split, smallest, largest):
    def one(axis_at, blocks):
        steps = jax.random.uniform(jax.random.fold_in(jax.random.fold_in(rng, 6), axis_at), (blocks,), jnp.float32, smallest / len(split), largest / len(split))
        return jnp.repeat(jnp.exp(steps), extent[axis_at] // blocks).reshape((-1,) + (1,) * (len(extent) - axis_at - 1))

    gain = one(*split[0])
    for cut in split[1:]:
        gain = gain * one(*cut)
    return gain


def gaussian(rng, dims, scale, reach, cuts=(), kind=jnp.bfloat16):
    array = scale * jax.random.normal(rng, dims, jnp.float32)
    if cuts:
        array = array * block_scale(rng, dims, cuts, -0.22, 0.18)
    return jnp.clip(array, -reach, reach).astype(kind)


def setup_inputs(seed: int = 0) -> dict:
    streams_of = jax.random.split(jax.random.key(seed), 8)
    queries = draw_queries(jax.random.fold_in(streams_of[7], 71), 0)
    key_rows = draw_key_rows(jax.random.fold_in(streams_of[7], 71), 0)
    values = gaussian(streams_of[2], (KEY_TOKENS, QUERY_FEATURES), 1.0, 6.0, ((0, 64), (1, 4)))
    w_out = gaussian(streams_of[3], (QUERY_FEATURES, D), 0.2, 1.1953125, ((0, 4),))
    picked = draw_picked(jax.random.fold_in(streams_of[7], 71), 0)
    counts = draw_counts(jax.random.fold_in(streams_of[7], 71), 0)
    tile_home = draw_tile_home(jax.random.fold_in(streams_of[7], 71), 0)
    return {"queries": queries, "key_rows": key_rows, "values": values, "w_out": w_out, "picked": picked, "counts": counts, "tile_home": tile_home}


def reference(queries, key_rows, values, w_out, picked, counts, tile_home):
    width = queries.shape[1]
    head_total = width // HD
    key_tiles = key_rows.reshape(NKT, TILE_TOKENS, width)
    value_tiles = values.reshape(NKT, TILE_TOKENS, width)
    scale = HD ** -0.5

    def attend(tile_index):
        query_tile = lax.dynamic_slice_in_dim(queries, tile_index * TILE_TOKENS, TILE_TOKENS, 0)
        query_tile = query_tile.astype(jnp.float32).reshape(TILE_TOKENS, head_total, HD)
        blocks = tile_home[picked[tile_index]]
        gathered_keys = key_tiles[blocks].astype(jnp.float32).reshape(MAXSEL * TILE_TOKENS, head_total, HD)
        gathered_values = value_tiles[blocks].astype(jnp.float32).reshape(MAXSEL * TILE_TOKENS, head_total, HD)
        logit_scores = jnp.einsum("qhd,khd->hqk", query_tile, gathered_keys) * scale
        is_live = (jnp.arange(MAXSEL * TILE_TOKENS, dtype=jnp.int32) // TILE_TOKENS) < counts[tile_index]
        logit_scores = jnp.where(is_live, logit_scores, -1e30)
        row_top = jnp.max(logit_scores, axis=-1, keepdims=True)
        exponent = jnp.where(is_live, jnp.exp(logit_scores - row_top), 0.0)
        row_sum_total = jnp.sum(exponent, axis=-1)
        weights = lax.optimization_barrier(exponent.astype(jnp.bfloat16)).astype(jnp.float32)
        mixed = jnp.einsum("hqk,khd->qhd", weights, gathered_values) / jnp.transpose(row_sum_total)[:, :, None]
        return mixed.reshape(TILE_TOKENS, width).astype(jnp.bfloat16)

    attended = lax.map(attend, jnp.arange(NQT, dtype=jnp.int32)).reshape(NQ, width)
    group = width // N_HEAD
    result = jnp.zeros((NQ, D), jnp.float32)
    for index in range(N_HEAD):
        part = jnp.dot(attended[:, index * group:(index + 1) * group], w_out[index * group:(index + 1) * group], preferred_element_type=jnp.float32)
        result = result + lax.optimization_barrier(part.astype(jnp.bfloat16)).astype(jnp.float32)
    return result.astype(jnp.bfloat16)
```

```python
import functools

import jax
import jax.numpy as jnp
from jax import lax
from jax.experimental import pallas as pl
from jax.experimental.pallas import tpu as pltpu
from jax.sharding import Mesh, PartitionSpec as P

HD = 128
MAXSEL = 24
TILE = 64
NX, NZ, NY, NC = 4, 8, 4, 2
KT_DEV = 12
ROW_TILES = NY * NC * KT_DEV
QT = NZ * NX
GROUP = NX * TILE
MAX_DUO = 96
UNROLL = 4
CHUNKS = 3
FEAT = 2 * HD
LOG2E = 1.4426950408889634
SCALE = HD ** -0.5 * LOG2E
NEG = -1e30


def shift(array, axis, size, by):
    return lax.ppermute(array, axis, [(i, (i + by) % size) for i in range(size)])


def route_kernel(pick_ref, count_ref, slot_ref, where_ref, table_ref):
    x, z, inner = where_ref[0], where_ref[1], where_ref[2]

    def per_query(q, base):
        group = (q // NX + z) % NZ
        tile = ((x - q % NX) % NX) * (NZ * NY * NC) + group * (NY * NC) + inner

        def per_pick(k, n):
            slot = slot_ref[pick_ref[k, tile]]
            table_ref[2 * base + n] = slot
            return n + (slot >= 0).astype(jnp.int32)

        n = lax.fori_loop(0, count_ref[tile], per_pick, 0)
        duos = (n + 1) // 2
        odd = n % 2

        @pl.when(odd == 1)
        def _():
            table_ref[2 * base + n] = table_ref[2 * base + n - 1]

        def mark(d, _):
            full = jnp.where((d == duos - 1) & (odd == 1), 0, 1)
            table_ref[2 * MAX_DUO + base + d] = 2 * q + full
            return 0

        lax.fori_loop(0, duos, mark, 0)
        return base + duos

    total = lax.fori_loop(0, QT, per_query, 0)
    for u in range(UNROLL - 1):
        table_ref[2 * MAX_DUO + total + u] = 2 * QT
        table_ref[2 * (total + u)] = 0
        table_ref[2 * (total + u) + 1] = 0
    table_ref[3 * MAX_DUO] = (total + UNROLL - 1) // UNROLL


def route(picked, counts, tile_home, x, z, y, c):
    inside = tile_home - z * ROW_TILES
    owner = inside // KT_DEV
    slot = (((owner // NC - y) % NY) * NC + ((owner % NC) ^ c)) * KT_DEV + inside % KT_DEV
    slot = jnp.where((inside >= 0) & (inside < ROW_TILES), slot, -1).astype(jnp.int32)
    where = jnp.stack([x, z, y * NC + c]).astype(jnp.int32)
    smem = pl.BlockSpec(memory_space=pltpu.SMEM)
    return pl.pallas_call(
        route_kernel,
        out_shape=jax.ShapeDtypeStruct((3 * MAX_DUO + 8,), jnp.int32),
        in_specs=[smem] * 4,
        out_specs=smem,
        name="route",
    )(picked.T, counts, slot, where)


def attend_kernel(table_ref, *refs):
    kv_in, q_in, outs = refs[:10], refs[10:19], refs[19:19 + NZ]
    kv, qs, acc, top, total, sem = refs[19 + NZ:]
    rows = KT_DEV * TILE
    half = rows // 2
    copies = []

    def fetch(src, dst):
        copies.append(pltpu.make_async_copy(src, dst, sem.at[len(copies)]))
        copies[-1].start()

    for dc in range(2):
        own, back, ahead, far0, far1 = kv_in[5 * dc:5 * dc + 5]
        for dy, src in ((0, own), (3, back), (1, ahead)):
            fetch(src, kv.at[pl.ds((dy * NC + dc) * rows, rows)])
        fetch(far0, kv.at[pl.ds((2 * NC + dc) * rows, half)])
        fetch(far1, kv.at[pl.ds((2 * NC + dc) * rows + half, half)])
    for k in range(7):
        fetch(q_in[k], qs.at[pl.ds((0, 7, 1, 6, 2, 5, 3)[k] * GROUP, GROUP)])
    fetch(q_in[7], qs.at[pl.ds(4 * GROUP, GROUP // 2)])
    fetch(q_in[8], qs.at[pl.ds(4 * GROUP + GROUP // 2, GROUP // 2)])
    acc[...] = jnp.zeros_like(acc)
    top[...] = jnp.full_like(top, NEG)
    total[...] = jnp.zeros_like(total)
    for copy in copies:
        copy.wait()
    lane = lax.broadcasted_iota(jnp.int32, (2 * TILE, 2 * TILE), 1)
    nt = (((1,), (1,)), ((), ()))

    def step(it, _):
        parts = []
        for u in range(UNROLL):
            d = it * UNROLL + u
            code = table_ref[2 * MAX_DUO + d]
            q = code // 2
            limit = jnp.where(code % 2 == 1, 2 * TILE, TILE)
            r1 = pl.multiple_of(table_ref[2 * d] * TILE, TILE)
            r2 = pl.multiple_of(table_ref[2 * d + 1] * TILE, TILE)
            rq = pl.multiple_of(jnp.minimum(q, QT - 1) * TILE, TILE)
            query = qs[pl.ds(rq, TILE), :]
            pair = jnp.concatenate([kv[pl.ds(r1, TILE), :], kv[pl.ds(r2, TILE), :]], axis=0)
            scores = jnp.concatenate([
                lax.dot_general(query[:, h * HD:(h + 1) * HD], pair[:, h * HD:(h + 1) * HD], nt,
                                preferred_element_type=jnp.float32)
                for h in range(2)
            ], axis=0)
            scores = jnp.where(lane < limit, scores, NEG)
            row_top = jnp.max(scores, axis=1, keepdims=True)
            exponent = jnp.exp2((scores - row_top) * SCALE)
            row_sum = jnp.sum(exponent, axis=1, keepdims=True)
            weights = exponent.astype(jnp.bfloat16)
            mixed = [
                jnp.dot(weights[h * TILE:(h + 1) * TILE], pair[:, FEAT + h * HD:FEAT + (h + 1) * HD],
                        preferred_element_type=jnp.float32)
                for h in range(2)
            ]
            parts.append((q, row_top, row_sum, mixed))
        for q, row_top, row_sum, mixed in parts:
            at = pl.ds(pl.multiple_of(q * TILE, TILE), TILE)
            for h in range(2):
                cols = pl.ds(h * HD, HD)
                mine = slice(h * TILE, (h + 1) * TILE)
                old = top[at, cols]
                fresh = jnp.broadcast_to(row_top[mine], (TILE, HD))
                new = jnp.maximum(old, fresh)
                keep = jnp.exp2((old - new) * SCALE)
                add = jnp.exp2((fresh - new) * SCALE)
                top[at, cols] = new
                total[at, cols] = total[at, cols] * keep + row_sum[mine] * add
                acc[at, cols] = acc[at, cols] * keep + mixed[h] * add
        return 0

    lax.fori_loop(0, table_ref[3 * MAX_DUO], step, 0)
    slot = lax.broadcasted_iota(jnp.int32, (GROUP, HD), 1)
    for k in range(NZ):
        at = pl.ds(k * GROUP, GROUP)
        stats = jnp.zeros((GROUP, HD), jnp.float32)
        for h in range(2):
            cols = pl.ds(h * HD, HD)
            count = total[at, cols]
            count = jnp.where(count > 0, count, 1.0)
            outs[k][pl.ds(0, GROUP), cols] = (acc[at, cols] / count).astype(jnp.bfloat16)
            logsum = top[at, cols] * SCALE + jnp.log2(count)
            high = logsum.astype(jnp.bfloat16).astype(jnp.float32)
            rest = logsum - high
            mid = rest.astype(jnp.bfloat16).astype(jnp.float32)
            low = rest - mid
            for p, piece in enumerate((high, mid, low)):
                stats = jnp.where(slot == 3 * h + p, piece, stats)
        outs[k][pl.ds(GROUP, 16), :] = stats.T[:16].astype(jnp.bfloat16)


def attend(table, kv_in, q_in):
    any_space = pl.BlockSpec(memory_space=pl.ANY)
    vmem = pl.BlockSpec(memory_space=pltpu.VMEM)
    return pl.pallas_call(
        attend_kernel,
        out_shape=[jax.ShapeDtypeStruct((GROUP + 16, FEAT), jnp.bfloat16)] * NZ,
        in_specs=[pl.BlockSpec(memory_space=pltpu.SMEM)] + [any_space] * 19,
        out_specs=[vmem] * NZ,
        scratch_shapes=[
            pltpu.VMEM((ROW_TILES * TILE, 2 * FEAT), jnp.bfloat16),
            pltpu.VMEM((QT * TILE, FEAT), jnp.bfloat16),
            pltpu.VMEM(((QT + 1) * TILE, FEAT), jnp.float32),
            pltpu.VMEM(((QT + 1) * TILE, FEAT), jnp.float32),
            pltpu.VMEM(((QT + 1) * TILE, FEAT), jnp.float32),
            pltpu.SemaphoreType.DMA((19,)),
        ],
        compiler_params=pltpu.CompilerParams(vmem_limit_bytes=32 << 20),
        cost_estimate=pl.CostEstimate(flops=1 << 32, bytes_accessed=10 << 20, transcendentals=1 << 20),
        name="attend",
    )(table, *kv_in, *q_in)


def merge_kernel(*refs):
    blocks, out = refs[:NZ], refs[NZ]
    logs = []
    for block in blocks:
        raw = block[pl.ds(GROUP, 16), :].astype(jnp.float32)
        logs.append([raw[3 * h:3 * h + 1] + raw[3 * h + 1:3 * h + 2] + raw[3 * h + 2:3 * h + 3] for h in range(2)])
    columns = []
    for h in range(2):
        top = functools.reduce(jnp.maximum, [log[h] for log in logs])
        parts = [jnp.exp2(log[h] - top) for log in logs]
        scale = 1.0 / functools.reduce(jnp.add, parts)
        columns += [part * scale for part in parts]
    table = jnp.concatenate(columns + [jnp.zeros((HD - 2 * NZ, GROUP), jnp.float32)], axis=0).T
    for h in range(2):
        cols = pl.ds(h * HD, HD)
        mixed = jnp.zeros((GROUP, HD), jnp.float32)
        for k in range(NZ):
            at = h * NZ + k
            mixed += blocks[k][pl.ds(0, GROUP), cols].astype(jnp.float32) * table[:, at:at + 1]
        out[:, cols] = mixed.astype(jnp.bfloat16)


def merge(blocks):
    vmem = pl.BlockSpec(memory_space=pltpu.VMEM)
    return pl.pallas_call(
        merge_kernel,
        out_shape=jax.ShapeDtypeStruct((GROUP, FEAT), jnp.bfloat16),
        in_specs=[vmem] * NZ,
        out_specs=vmem,
        cost_estimate=pl.CostEstimate(flops=1 << 22, bytes_accessed=2 << 20, transcendentals=1 << 13),
        name="merge",
    )(*blocks)


def body(queries, key_rows, values, w_out, picked, counts, tile_home):
    x, z, y, c = (lax.axis_index(name) for name in ("x", "z", "y", "c"))
    width = w_out.shape[0]
    half = KT_DEV * TILE // 2
    table = route(picked, counts, tile_home, x, z, y, c)

    def columns(k):
        return lax.dynamic_slice_in_dim(queries, (x + k) % NX * width, width, 1)

    mine = [columns(0)] + [shift(columns(k), "x", NX, k) for k in range(1, NX)]
    local_queries = jnp.concatenate(mine, axis=0)

    merged = []
    for chunk in range(CHUNKS):
        cols = slice(chunk * FEAT, (chunk + 1) * FEAT)
        own = jnp.concatenate([key_rows[:, cols], values[:, cols]], axis=1)
        back, ahead = shift(own, "y", NY, 1), shift(own, "y", NY, -1)
        far0, far1 = shift(back[:half], "y", NY, 1), shift(ahead[half:], "y", NY, -1)
        kv_in = [own, back, ahead, far0, far1]
        kv_in += [shift(block, "c", NC, 1) for block in kv_in]
        q_own = local_queries[:, cols]
        q_in = [q_own]
        left = right = q_own
        for _ in range(3):
            right, left = shift(right, "z", NZ, 1), shift(left, "z", NZ, -1)
            q_in += [right, left]
        q_in.append(shift(right[:GROUP // 2], "z", NZ, 1))
        q_in.append(shift(left[GROUP // 2:], "z", NZ, -1))
        outs = attend(table, kv_in, q_in)
        blocks = [outs[0]] + [shift(outs[k], "z", NZ, k) for k in (4, 3, 5, 2, 6, 1, 7)]
        merged.append(merge(blocks))
    attended = jnp.concatenate(merged, axis=1)
    partial = jnp.dot(attended, w_out, preferred_element_type=jnp.float32).astype(jnp.bfloat16)
    summed = partial[:TILE].astype(jnp.float32)
    for k in range(1, NX):
        summed += shift(partial[k * TILE:(k + 1) * TILE], "x", NX, -k).astype(jnp.float32)
    return summed.astype(jnp.bfloat16)


def solution(mesh):
    torus = Mesh(mesh.devices.reshape(NX, NZ, NY, NC), ("x", "z", "y", "c"))
    seq = ("z", "y", "c")
    placed = (
        P(("x",) + seq, None),
        P(seq, "x"),
        P(seq, "x"),
        P("x", None),
        P(),
        P(),
        P(),
    )
    return jax.shard_map(
        body, mesh=torus, in_specs=placed, out_specs=P(("x",) + seq, None), check_vma=False
    )
```
